256 devices in a mesh: section: 32 (over y, z_hi, core), band: 8 (over x, z_lo).
Axes of the slice: x: 4, y: 4, z: 8 (z_hi: 4, z_lo: 2; z = z_hi * 2 + z_lo), core: 2. Of those that a mesh axis runs over, the one named last changes fastest.
Arguments:
- section_inputs: bfloat16 [32, 2, 64, 64, 256], P('section', None, 'band'), may hold values from -6 to 6
- skip_inputs: bfloat16 [32, 2, 64, 64, 256], P('section', None, 'band'), may hold values from -6 to 6
- fresh_batches: bfloat16 [2, 2, 64, 64, 256], P(None, None, 'band'), may hold values from -6 to 6
- first_weights: bfloat16 [32, 3, 3, 256, 256], P('section'), may hold values from -0.1875 to 0.1875
- skip_weights: bfloat16 [32, 3, 3, 256, 256], P('section'), may hold values from -0.1875 to 0.1875
- second_weights: bfloat16 [32, 3, 3, 256, 256], P('section'), may hold values from -0.1875 to 0.1875
Outputs:
- produced: bfloat16 [32, 2, 64, 64, 256], P('section', None, 'band')
- mirrored: bfloat16 [32, 2, 64, 64, 256], P('section', None, 'band')
The draws below stay inside these ranges and needn't reach their ends.
All inputs are finite; a program needn't handle non-finite values.
Results may differ from the reference program's by a relative error of at most 0.012.
Values may be sent and summed in bfloat16 or wider, within the bound.
No kernel may reach another device: no remote copies, remote signals or barrier semaphores. Data moves between devices by JAX's collectives and lax.ppermute only.
A program may use at most 64 MiB of HBM per device.

```python
import jax
import jax.numpy as jnp
from jax import lax

C = 256
WIDTH = 64
MB = 2
TICKS = 3
SECTIONS = 32
HEIGHT = 64


def level_of(key, shape, pieces, low, top_value):
    factor_of = 1.0
    for dim, parts in pieces:
        steps = jax.random.uniform(jax.random.fold_in(jax.random.fold_in(key, 6), dim), (parts,), jnp.float32, low / len(pieces), top_value / len(pieces))
        factor_of = factor_of * jnp.repeat(jnp.exp(steps), shape[dim] // parts).reshape((-1,) + (1,) * (len(shape) - 1 - dim))
    return factor_of


def centred(own_key, dims, spread, bound, shards=(), dtype=jnp.bfloat16):
    entries = jax.random.normal(own_key, dims, jnp.float32) * spread
    if len(shards) > 0:
        entries = level_of(own_key, dims, shards, -0.22, 0.18) * entries
    return jnp.clip(entries, min=-bound, max=bound).astype(dtype)


def setup_inputs(seed: int = 0) -> dict:
    splits = jax.random.split(jax.random.key(seed), 7)
    return {
        "section_inputs": centred(splits[0], (SECTIONS, MB, HEIGHT, WIDTH, C), 1.0, 6.0, ((0, 32), (2, 8))),
        "skip_inputs": centred(splits[1], (SECTIONS, MB, HEIGHT, WIDTH, C), 1.0, 6.0, ((0, 32), (2, 8))),
        "fresh_batches": centred(splits[2], (TICKS - 1, MB, HEIGHT, WIDTH, C), 1.0, 6.0, ((2, 8),)),
        "first_weights": centred(splits[3], (SECTIONS, 3, 3, C, C), ((2.0 / (9 * C)) ** 0.5), 0.1875, ((0, 32),)),
        "skip_weights": centred(splits[4], (SECTIONS, 3, 3, C, C), ((2.0 / (9 * C)) ** 0.5), 0.1875, ((0, 32),)),
        "second_weights": centred(splits[5], (SECTIONS, 3, 3, C, C), ((2.0 / (9 * C)) ** 0.5), 0.1875, ((0, 32),)),
    }


def conv_rows(padded, weight, out_rows):
    width = padded.shape[2]
    wide = jnp.pad(padded, ((0, 0), (0, 0), (1, 1), (0, 0)))
    total = jnp.zeros((padded.shape[0], out_rows, width, weight.shape[3]), jnp.float32)
    for row_shift in range(3):
        for col_shift in range(3):
            window = wide[:, row_shift:row_shift + out_rows, col_shift:col_shift + width, :]
            flat = window.reshape(-1, window.shape[3])
            product = jnp.dot(flat, weight[row_shift, col_shift], preferred_element_type=jnp.float32)
            total = total + product.reshape(total.shape)
    return total


def section_block(current, mirrored, first_weight, skip_weight, second_weight, decoder):
    rows = current.shape[1]
    pad_rows = ((0, 0), (1, 1), (0, 0), (0, 0))
    first_sum = conv_rows(jnp.pad(current, pad_rows), first_weight, rows)
    first_sum = first_sum + decoder * conv_rows(jnp.pad(mirrored, pad_rows), skip_weight, rows)
    hidden = jax.nn.relu(first_sum).astype(jnp.bfloat16)
    second_sum = conv_rows(jnp.pad(hidden, pad_rows), second_weight, rows)
    return jax.nn.relu(second_sum).astype(jnp.bfloat16)


def reference(section_inputs, skip_inputs, fresh_batches, first_weights, skip_weights, second_weights):
    sections = first_weights.shape[0]
    decoder_flags = (jnp.arange(sections) >= sections // 2).astype(jnp.float32)
    current = section_inputs
    mirrored = skip_inputs
    produced = section_inputs
    for tick_index in range(TICKS):
        produced = lax.map(lambda items: section_block(*items), (current, mirrored, first_weights, skip_weights, second_weights, decoder_flags))
        mirrored = produced[::-1]
        if tick_index + 1 < TICKS:
            current = jnp.concatenate([fresh_batches[tick_index][None], produced[:-1]], axis=0)
    return produced, mirrored
```

```python
import jax
import jax.numpy as jnp
from jax import lax
from jax.sharding import PartitionSpec as P

TICKS = 3


def conv(rows, weight):
    return lax.conv_general_dilated(
        rows,
        weight,
        (1, 1),
        ((0, 0), (1, 1)),
        dimension_numbers=("NHWC", "HWIO", "NHWC"),
        preferred_element_type=jnp.float32,
    )


def halo(head, tail):
    count = lax.axis_size("band")
    ends = range(count - 1)
    above = lax.ppermute(tail, "band", [(i, i + 1) for i in ends])
    below = lax.ppermute(head, "band", [(i + 1, i) for i in ends])
    return above, below


def body(section_inputs, skip_inputs, fresh_batches, first_weights, skip_weights, second_weights):
    sections = lax.axis_size("section")
    bands = lax.axis_size("band")
    section_index = lax.axis_index("section")
    band_index = lax.axis_index("band")
    is_decoder = section_index >= sections // 2
    first_weight = first_weights[0]
    skip_weight = skip_weights[0]
    second_weight = second_weights[0]
    current = section_inputs[0]
    rows = current.shape[1]
    to_next = [(s, s + 1) for s in range(sections - 1)]
    to_decoder = [(s, sections - 1 - s) for s in range(sections // 2)]
    to_mirror = [(s, sections - 1 - s) for s in range(sections)]
    row = lax.broadcasted_iota(jnp.int32, (1, rows + 2, 1, 1), 1)
    inside = ((row > 0) | (band_index > 0)) & ((row < rows + 1) | (band_index < bands - 1))

    skip = jnp.where(is_decoder, skip_inputs[0], jnp.zeros((), jnp.bfloat16))
    head, inner, tail = skip[:, :2], skip[:, 2:-2], skip[:, -2:]
    for tick_index in range(TICKS):
        above, below = halo(current[:, :2], current[:, -2:])
        skip_above, skip_below = halo(head, tail)
        first_sum = conv(jnp.concatenate([above, current, below], axis=1), first_weight)
        padded = jnp.concatenate([skip_above, head, inner, tail, skip_below], axis=1)
        first_sum = first_sum + conv(padded, skip_weight)
        hidden = jnp.where(inside, jax.nn.relu(first_sum), 0.0).astype(jnp.bfloat16)
        produced = jax.nn.relu(conv(hidden, second_weight)).astype(jnp.bfloat16)
        if tick_index + 1 < TICKS:
            arriving = lax.ppermute(produced, "section", to_next)
            edges = jnp.concatenate([produced[:, :2], produced[:, -2:]], axis=1)
            edges = lax.ppermute(edges, "section", to_decoder)
            inner = lax.ppermute(produced[:, 2:-2], "section", to_decoder)
            head, tail = edges[:, :2], edges[:, 2:]
            current = jnp.where(section_index == 0, fresh_batches[tick_index], arriving)
    mirrored = lax.ppermute(produced, "section", to_mirror)
    return (produced[None], mirrored[None])


def solution(mesh):
    in_specs = (
        P("section", None, "band", None, None),
        P("section", None, "band", None, None),
        P(None, None, "band", None, None),
        P("section", None, None, None, None),
        P("section", None, None, None, None),
        P("section", None, None, None, None),
    )
    out_specs = (P("section", None, "band", None, None), P("section", None, "band", None, None))
    return jax.shard_map(body, mesh=mesh, in_specs=in_specs, out_specs=out_specs, check_vma=False)
```

```python
import jax
import jax.numpy as jnp
from jax import lax
from jax.experimental import pallas as pl
from jax.experimental.pallas import tpu as pltpu
from jax.sharding import PartitionSpec as P

TICKS = 3
HALO = 2


def conv_into(rows_ref, weight_ref, sums_ref, rows, fresh):
    width, depth = rows_ref.shape[1], rows_ref.shape[2]
    for b in range(3):
        total = None
        for a in range(3):
            lhs = rows_ref[a : a + rows].reshape(rows * width, depth)
            term = jnp.dot(lhs, weight_ref[a, b], preferred_element_type=jnp.float32)
            total = term if total is None else total + term
        total = total.reshape(rows, width, -1)
        if fresh:
            sums_ref[b, :rows] = total
        else:
            sums_ref[b, :rows] = sums_ref[b, :rows] + total


def folded(sums_ref, rows):
    width, depth = sums_ref.shape[2], sums_ref.shape[3]
    column = lax.broadcasted_iota(jnp.int32, (rows, width, depth), 1)
    left = pltpu.roll(sums_ref[0, :rows], 1, axis=1)
    right = pltpu.roll(sums_ref[2, :rows], width - 1, axis=1)
    left = jnp.where(column == 0, 0.0, left)
    right = jnp.where(column == width - 1, 0.0, right)
    return jnp.maximum(sums_ref[1, :rows] + left + right, 0.0)


def tick_kernel(
    last, flags_ref, edge_ref, inner_ref, far_ref, skip_edge_ref, skip_inner_ref, skip_far_ref,
    first_ref, skip_ref, second_ref, *refs,
):
    outs, (rows_ref, skip_rows_ref, hidden_ref, sums_ref) = refs[:-4], refs[-4:]
    images, inner = inner_ref.shape[0], inner_ref.shape[1]
    rows = inner + 2 * HALO

    def fill(target, edge, middle, far, image):
        target[:HALO] = far[0, image]
        target[HALO : 2 * HALO] = edge[0, image]
        target[2 * HALO : 2 * HALO + inner] = middle[image]
        target[2 * HALO + inner : 3 * HALO + inner] = edge[1, image]
        target[3 * HALO + inner :] = far[1, image]

    def one(image, carry):
        fill(rows_ref, edge_ref, inner_ref, far_ref, image)
        fill(skip_rows_ref, skip_edge_ref, skip_inner_ref, skip_far_ref, image)
        conv_into(rows_ref, first_ref, sums_ref, rows + 2, True)
        conv_into(skip_rows_ref, skip_ref, sums_ref, rows + 2, False)
        hidden_ref[...] = folded(sums_ref, rows + 2).astype(jnp.bfloat16)
        for place, flag in ((0, 0), (rows + 1, 1)):

            @pl.when(flags_ref[flag] == 0)
            def _():
                hidden_ref[place] = jnp.zeros(hidden_ref.shape[1:], jnp.bfloat16)

        conv_into(hidden_ref, second_ref, sums_ref, rows, True)
        produced = folded(sums_ref, rows).astype(jnp.bfloat16)
        if last:
            outs[0][image] = produced
        else:
            outs[0][0, image] = produced[:HALO]
            outs[0][1, image] = produced[HALO + inner :]
            outs[1][image] = produced[HALO : HALO + inner]
        return carry

    lax.fori_loop(0, images, one, 0)


def run_tick(last, flags, edge, inner, far, skip_edge, skip_inner, skip_far, *weights):
    images, middle, width, depth = inner.shape
    rows = middle + 2 * HALO
    kind = jnp.bfloat16
    if last:
        out_shape = (jax.ShapeDtypeStruct((images, rows, width, depth), kind),)
    else:
        out_shape = (jax.ShapeDtypeStruct(edge.shape, kind), jax.ShapeDtypeStruct(inner.shape, kind))
    vmem = pl.BlockSpec(memory_space=pltpu.VMEM)
    flops = 2 * images * width * 9 * depth * depth * (2 * (rows + 2) + rows)
    return pl.pallas_call(
        lambda *refs: tick_kernel(last, *refs),
        out_shape=out_shape,
        in_specs=[pl.BlockSpec(memory_space=pltpu.SMEM)] + [vmem] * 9,
        out_specs=(vmem,) * len(out_shape),
        scratch_shapes=[
            pltpu.VMEM((rows + 2 * HALO, width, depth), kind),
            pltpu.VMEM((rows + 2 * HALO, width, depth), kind),
            pltpu.VMEM((rows + 2, width, depth), kind),
            pltpu.VMEM((3, rows + 2, width, depth), jnp.float32),
        ],
        compiler_params=pltpu.CompilerParams(vmem_limit_bytes=24 * 1024 * 1024),
        cost_estimate=pl.CostEstimate(flops=flops, bytes_accessed=8 * 1024 * 1024, transcendentals=0),
        name="last_tick" if last else "tick",
    )(flags, edge, inner, far, skip_edge, skip_inner, skip_far, *weights)


def body(section_inputs, skip_inputs, fresh_batches, first_weights, skip_weights, second_weights):
    sections = lax.axis_size("section")
    bands = lax.axis_size("band")
    section_index = lax.axis_index("section")
    band_index = lax.axis_index("band")
    half = sections // 2
    is_decoder = section_index >= half
    is_first = section_index == 0
    weights = (
        first_weights[0],
        jnp.where(is_decoder, skip_weights[0], jnp.zeros((), jnp.bfloat16)),
        second_weights[0],
    )
    flags = jnp.stack([band_index > 0, band_index < bands - 1]).astype(jnp.int32)
    to_next = [(s, s + 1) for s in range(sections - 1)]
    to_decoder = [(s, sections - 1 - s) for s in range(half)]
    to_mirror = [(s, sections - 1 - s) for s in range(sections)]

    def split(value):
        edge = jnp.stack([value[:, :HALO], value[:, -HALO:]])
        return edge, value[:, HALO:-HALO]

    def halo(edge, of):
        ends = [(s * bands + i, s * bands + i + 1) for s in of for i in range(bands - 1)]
        axes = ("section", "band")
        above = lax.ppermute(edge[1], axes, ends)
        below = lax.ppermute(edge[0], axes, [(j, i) for i, j in ends])
        return jnp.stack([above, below])

    edge, inner = split(section_inputs[0])
    skip_edge, skip_inner = split(skip_inputs[0])
    for tick_index in range(TICKS):
        far = halo(edge, range(sections))
        skip_far = halo(skip_edge, range(half, sections))
        last = tick_index + 1 == TICKS
        outs = run_tick(last, flags, edge, inner, far, skip_edge, skip_inner, skip_far, *weights)
        if not last:
            fresh_edge, fresh_inner = split(fresh_batches[tick_index])
            edge = lax.ppermute(outs[0], "section", to_next)
            skip_edge = lax.ppermute(outs[0], "section", to_decoder)
            inner = lax.ppermute(outs[1], "section", to_next)
            skip_inner = lax.ppermute(outs[1], "section", to_decoder)
            edge = jnp.where(is_first, fresh_edge, edge)
            inner = jnp.where(is_first, fresh_inner, inner)
    produced = outs[0]
    mirrored = lax.ppermute(produced, "section", to_mirror)
    return (produced[None], mirrored[None])


def solution(mesh):
    in_specs = (
        P("section", None, "band", None, None),
        P("section", None, "band", None, None),
        P(None, None, "band", None, None),
        P("section", None, None, None, None),
        P("section", None, None, None, None),
        P("section", None, None, None, None),
    )
    out_specs = (P("section", None, "band", None, None), P("section", None, "band", None, None))
    return jax.shard_map(body, mesh=mesh, in_specs=in_specs, out_specs=out_specs, check_vma=False)
```
